128 devices in a mesh: inp: 16 (over y, x_lo, core), spec: 8 (over x_hi, z).
Axes of the slice: x: 4 (x_hi: 2, x_lo: 2; x = x_hi * 2 + x_lo), y: 4, z: 4, core: 2. Of those that a mesh axis runs over, the one named last changes fastest.
Arguments:
- voltages: bfloat16 [2048, 262144], P('inp', 'spec'), may hold values from -6 to 6
Outputs:
- visibilities: float32 [128, 136, 2, 128, 128], P(('inp', 'spec'))
The draws below stay inside these ranges and needn't reach their ends.
All inputs are finite; a program needn't handle non-finite values.
Results may differ from the reference program's by a relative error of at most 0.0054.
Values may be sent and summed in bfloat16 or wider, within the bound.
A program may use at most 128 MiB of HBM per device.

```python
import math
import jax
import jax.numpy as jnp
import numpy as np
from jax import lax

NI = 2048
NFFT = 2048
NTAP = 4
TB = 128
NSPEC = 128
NSAMP = 262144
CHANS = 128
STEP = 8
N_INP = 16


def levels(key, extent, shards, least, high):
    def one(axis_at, shards_of):
        steps = jax.random.uniform(jax.random.fold_in(jax.random.fold_in(key, 6), axis_at), (shards_of,), jnp.float32, least / len(shards), high / len(shards))
        return jnp.repeat(jnp.exp(steps), extent[axis_at] // shards_of).reshape((-1,) + (1,) * (len(extent) - axis_at - 1))

    gain = one(*shards[0])
    for cut in shards[1:]:
        gain = gain * one(*cut)
    return gain


def gaussian(rng, shape, scale, reach, cuts=(), held_as=jnp.bfloat16):
    loudness = levels(rng, shape, cuts, -0.22, 0.18) if cuts else 1.0
    values = jax.random.normal(rng, shape, jnp.float32) * scale * loudness
    return jnp.minimum(jnp.maximum(values, -reach), reach).astype(held_as)


def setup_inputs(seed: int = 0) -> dict:
    arg_keys = jax.random.split(jax.random.key(seed), 2)
    return {
        "voltages": gaussian(arg_keys[0], (NI, NSAMP), 1.0, 6.0, ((0, 16), (1, 8))),
    }


def window_taps(ntaps, nfft):
    sample_pos = jnp.arange(ntaps * nfft, dtype=jnp.float32)
    centered = (sample_pos - 0.5 * ntaps * nfft) / nfft
    hann_part = 0.5 - 0.5 * jnp.cos(sample_pos * (2.0 * math.pi / (ntaps * nfft)))
    return (jnp.sinc(centered) * hann_part).reshape(ntaps, nfft)

def dft_columns(nfft, chan_total, chan_step):
    sample_idx = jnp.arange(nfft, dtype=jnp.int32)
    chan_freq = jnp.arange(chan_total, dtype=jnp.int32) * chan_step + chan_step // 2
    phase_int = sample_idx[:, None] * chan_freq[None, :] % nfft
    phase_angle = phase_int.astype(jnp.float32) * (2.0 * math.pi / nfft)
    dft_norm = 1.0 / math.sqrt(nfft)
    stacked = jnp.stack([jnp.cos(phase_angle) * dft_norm, -jnp.sin(phase_angle) * dft_norm], axis=2)
    return stacked.reshape(nfft, 2 * chan_total)

def filter_kernel(ntaps, nfft, chan_total, chan_step):
    taps = window_taps(ntaps, nfft)
    columns = dft_columns(nfft, chan_total, chan_step)
    return (taps[:, :, None] * columns[None, :, :]).astype(jnp.bfloat16)

def reference(voltages):
    kernel = filter_kernel(NTAP, NFFT, CHANS, STEP).astype(jnp.float32)
    block_rows = NI // N_INP

    def channelize(rows):
        zero_lead = jnp.zeros((block_rows, (NTAP - 1) * NFFT), jnp.bfloat16)
        padded = jnp.concatenate([zero_lead, rows], axis=1).reshape(block_rows, NSPEC + NTAP - 1, NFFT)
        padded = padded.astype(jnp.float32)
        total = jnp.zeros((block_rows * NSPEC, 2 * CHANS), jnp.float32)
        for tap_index in range(NTAP):
            frames = padded[:, tap_index:tap_index + NSPEC].reshape(block_rows * NSPEC, NFFT)
            total = total + jnp.dot(frames, kernel[tap_index], precision=lax.Precision.HIGHEST)
        return total.astype(jnp.bfloat16)
    spectra = lax.map(channelize, voltages.reshape(N_INP, block_rows, NSAMP))
    per_chan = spectra.reshape(NI, NSPEC, CHANS, 2).transpose(2, 3, 1, 0)
    row_blocks = NI // TB
    row_index, col_index = np.triu_indices(row_blocks)

    def correlate(chan_block):
        stacked_rows = chan_block.reshape(2 * NSPEC, NI).astype(jnp.float32)
        turned = jnp.concatenate([-chan_block[1], chan_block[0]], axis=0).astype(jnp.float32)
        real_part = jnp.dot(stacked_rows.T, stacked_rows, precision=lax.Precision.HIGHEST)
        imag_part = jnp.dot(stacked_rows.T, turned, precision=lax.Precision.HIGHEST)
        pair_parts = jnp.stack([real_part, imag_part], axis=0) * (1.0 / NSPEC)
        tiled = pair_parts.reshape(2, row_blocks, TB, row_blocks, TB).transpose(1, 3, 0, 2, 4)
        return tiled[row_index, col_index]
    return lax.map(correlate, per_chan)
```

```python
import functools
import math

import jax
import jax.numpy as jnp
import numpy as np
import ml_dtypes
from jax import lax
from jax.experimental import pallas as pl
from jax.experimental.pallas import tpu as pltpu
from jax.sharding import PartitionSpec as P

NFFT = 2048
NTAP = 4
TB = 128
CHANS = 128
STEP = 8
FRAMES = 16
CHUNKS = 4
PER = CHANS // CHUNKS
ROWS = 2 * PER
LOGICAL = pl.DeviceIdType.LOGICAL


def filter_rows():
    pos = np.arange(NTAP * NFFT, dtype=np.float64)
    window = np.sinc((pos - 0.5 * NTAP * NFFT) / NFFT) * (0.5 - 0.5 * np.cos(2.0 * math.pi * pos / (NTAP * NFFT)))
    freq = np.arange(CHANS) * STEP + STEP // 2
    angle = (np.arange(NFFT)[:, None] * freq[None, :] % NFFT) * (2.0 * math.pi / NFFT)
    columns = np.stack([np.cos(angle), -np.sin(angle)], axis=2) / math.sqrt(NFFT)
    window = window.astype(np.float32).reshape(NTAP, NFFT, 1)
    columns = columns.astype(np.float32).reshape(1, NFFT, 2 * CHANS)
    kernel = (window * columns).astype(ml_dtypes.bfloat16)
    kernel = kernel.transpose(0, 2, 1).reshape(NTAP, CHUNKS, ROWS, NFFT)
    return np.ascontiguousarray(kernel.transpose(1, 0, 2, 3)).reshape(CHUNKS, NTAP * ROWS, NFFT)


def far_first():
    hops = lambda d: min(d, 4 - d)
    all_of = [(dx, dz, dc) for dx in range(4) for dz in range(4) for dc in range(2)]
    return sorted(all_of, key=lambda o: (-hops(o[0]) - hops(o[1]), -o[2], (o[0] * 7 + o[1] * 5) % 11))


def spread_kernel(v_ref, k_ref, r_ref, vbuf, kbuf, prod, acc, tail, out, vsem, ksem, ssem, rsem, lsem):
    a, b = lax.axis_index("inp"), lax.axis_index("spec")
    me = a * 8 + b
    y, x_lo, core = lax.div(a, 4), lax.rem(lax.div(a, 2), 2), lax.rem(a, 2)
    x, z = lax.div(b, 4) * 2 + x_lo, lax.rem(b, 4)

    def plane(c):
        return lax.rem(y + 2 + c - lax.div(c, 2) * (2 * c - 1), 4)

    def k_copy(c):
        return pltpu.make_async_copy(k_ref.at[plane(c)], kbuf.at[c], ksem.at[c])

    def v_copy(f):
        return pltpu.make_async_copy(v_ref.at[:, pl.ds(pl.multiple_of(f * NFFT, NFFT), NFFT)], vbuf.at[f], vsem.at[f])

    k_copy(0).start()
    for f in range(FRAMES):
        v_copy(f).start()
    for c in range(1, CHUNKS):
        k_copy(c).start()

    barrier = pltpu.get_barrier_semaphore()

    def greet(k, carry):
        pl.semaphore_signal(barrier, inc=1, device_id=lax.rem(me + k, 128), device_id_type=LOGICAL)
        return carry

    lax.fori_loop(1, 128, greet, 0)
    tail[...] = jnp.zeros_like(tail)

    def chunk(c, carry):
        k_copy(c).wait()

        def pair(g, carry):
            @pl.when(c == 0)
            def _():
                v_copy(2 * g).wait()
                v_copy(2 * g + 1).wait()

            frames = vbuf[pl.ds(2 * g, 2)].reshape(2 * 128, NFFT)
            got = lax.dot_general(kbuf[c], frames, (((1,), (1,)), ((), ())), preferred_element_type=jnp.float32)
            prod[2 * g] = got[:, :128]
            prod[2 * g + 1] = got[:, 128:]
            return carry

        lax.fori_loop(0, FRAMES // 2, pair, 0)

        def group(g, carry):
            for s in range(FRAMES + NTAP - 1):
                total = None
                for t in range(NTAP):
                    f = s + t - (NTAP - 1)
                    if 0 <= f < FRAMES:
                        term = prod[f, pl.ds(pl.multiple_of(t * ROWS + 8 * g, 8), 8), :]
                        total = term if total is None else total + term
                if s < FRAMES:
                    acc[pl.ds(8 * g * FRAMES + s, 8, stride=FRAMES), :] = total
                else:
                    tail[pl.ds(8 * g * 4 + s - FRAMES, 8, stride=4), :] = total
            return carry

        lax.fori_loop(0, ROWS // 8, group, 0)

        def pack(l, carry):
            for k in range(4):
                out[c, l, k] = acc[pl.ds(pl.multiple_of(l * 32 + k * 8, 8), 8), :].astype(jnp.bfloat16)
            out[c, l, 4] = tail[pl.ds(pl.multiple_of(l * 8, 8), 8), :].astype(jnp.bfloat16)
            return carry

        lax.fori_loop(0, PER, pack, 0)

        @pl.when(c == 0)
        def _():
            pl.semaphore_wait(barrier, 127)

        y_to = plane(c)

        def send(dx, dz, dc):
            x_to, z_to = lax.rem(x + dx, 4), lax.rem(z + dz, 4)
            l = (lax.rem(x_to, 2) * 2 + lax.rem(core + dc, 2)) * 8 + lax.div(x_to, 2) * 4 + z_to
            pltpu.make_async_remote_copy(
                src_ref=out.at[c, l],
                dst_ref=r_ref.at[me],
                send_sem=ssem,
                recv_sem=rsem,
                device_id=y_to * 32 + l,
                device_id_type=LOGICAL,
            ).start()

        for offset in far_first()[:-1]:
            send(*offset)

        @pl.when(c < CHUNKS - 1)
        def _():
            send(0, 0, 0)

        return carry

    lax.fori_loop(0, CHUNKS, chunk, 0)
    own = pltpu.make_async_copy(out.at[CHUNKS - 1, lax.rem(me, 32)], r_ref.at[me], lsem)
    own.start()
    own.wait()
    landed = r_ref.at[pl.ds(0, 127)]
    pltpu.make_async_copy(landed, landed, ssem).wait()
    pltpu.make_async_copy(landed, landed, rsem).wait()


def spread(v, kernel):
    return pl.pallas_call(
        spread_kernel,
        out_shape=jax.ShapeDtypeStruct((128, 5, 8, 128), jnp.bfloat16),
        in_specs=[pl.BlockSpec(memory_space=pl.ANY)] * 2,
        out_specs=pl.BlockSpec(memory_space=pltpu.VMEM),
        scratch_shapes=[
            pltpu.VMEM((FRAMES, 128, NFFT), jnp.bfloat16),
            pltpu.VMEM((CHUNKS, NTAP * ROWS, NFFT), jnp.bfloat16),
            pltpu.VMEM((FRAMES, NTAP * ROWS, 128), jnp.float32),
            pltpu.VMEM((ROWS * FRAMES, 128), jnp.float32),
            pltpu.VMEM((ROWS * 4, 128), jnp.float32),
            pltpu.VMEM((CHUNKS, PER, 5, 8, 128), jnp.bfloat16),
            pltpu.SemaphoreType.DMA((FRAMES,)),
            pltpu.SemaphoreType.DMA((CHUNKS,)),
            pltpu.SemaphoreType.DMA,
            pltpu.SemaphoreType.DMA,
            pltpu.SemaphoreType.DMA,
        ],
        compiler_params=pltpu.CompilerParams(collective_id=0, has_side_effects=True, vmem_limit_bytes=40 << 20),
        name="spread",
    )(v, kernel)


BLOCKS = 16
TILES = BLOCKS * (BLOCKS + 1) // 2


def tile_index(r, c):
    return r * BLOCKS - r * (r - 1) // 2 + (c - r)


def correlate_kernel(r_ref, o_ref, left, right, stage, sem):
    row = lax.broadcasted_iota(jnp.int32, (8, 128), 0)
    for c in range(BLOCKS):
        for part in range(2):
            for b in range(8):
                src = c * 8 + b
                head = r_ref[src, 2 * part].astype(jnp.float32)
                rest = r_ref[src, 2 * part + 1].astype(jnp.float32)
                if b > 0:
                    terms = r_ref[src - 1, 4].astype(jnp.float32)
                    if part == 1:
                        terms = jnp.concatenate([terms[4:], terms[:4]], axis=0)
                    head = head + jnp.where(row < NTAP - 1, terms, 0.0)
                both = jnp.concatenate([head, rest], axis=0)
                at = part * 128 + b * 16
                right[c % 2, pl.ds(at, 16), 0:128] = both.astype(jnp.bfloat16)
        re, im = right[c % 2, 0:128, 0:128], right[c % 2, 128:256, 0:128]
        right[c % 2, 0:128, 128:256] = -im
        right[c % 2, 128:256, 128:256] = re
        left[c * 128 : (c + 1) * 128, 0:128] = re.T
        left[c * 128 : (c + 1) * 128, 128:256] = im.T
        got = jnp.dot(left[0 : (c + 1) * 128, :], right[c % 2], preferred_element_type=jnp.float32)
        for r in range(c + 1):
            t = tile_index(r, c)
            stage[t, 0] = got[r * 128 : (r + 1) * 128, 0:128] * (1.0 / 128)
            stage[t, 1] = got[r * 128 : (r + 1) * 128, 128:256] * (1.0 / 128)
        for r in range(c + 1):
            t = tile_index(r, c)
            pltpu.make_async_copy(stage.at[t], o_ref.at[t], sem).start()
    pltpu.make_async_copy(stage, o_ref, sem).wait()


def correlate(got):
    return pl.pallas_call(
        correlate_kernel,
        out_shape=jax.ShapeDtypeStruct((TILES, 2, TB, TB), jnp.float32),
        in_specs=[pl.BlockSpec(memory_space=pltpu.VMEM)],
        out_specs=pl.BlockSpec(memory_space=pl.ANY),
        scratch_shapes=[
            pltpu.VMEM((BLOCKS * 128, 256), jnp.bfloat16),
            pltpu.VMEM((2, 256, 256), jnp.bfloat16),
            pltpu.VMEM((TILES, 2, TB, TB), jnp.float32),
            pltpu.SemaphoreType.DMA,
        ],
        compiler_params=pltpu.CompilerParams(vmem_limit_bytes=40 << 20),
        name="correlate",
    )(got)


def shards(voltages):
    got = spread(voltages, jnp.asarray(filter_rows()))
    return correlate(got)[None]


def solution(mesh):
    return jax.shard_map(
        shards,
        mesh=mesh,
        in_specs=(P("inp", "spec"),),
        out_specs=P(("inp", "spec"), None, None, None, None),
        check_vma=False,
    )
```

```python
import math
import random

import jax
import jax.numpy as jnp
from jax import lax
from jax.experimental import pallas as pl
from jax.experimental.pallas import tpu as pltpu
from jax.sharding import PartitionSpec as P

NFFT = 2048
NTAP = 4
TB = 128
CHANS = 128
STEP = 8
FRAMES = 16
HALF = FRAMES // 2
FOLD = 256
TURNS = NFFT // FOLD
GROUP = 32
BATCH = 16
LOGICAL = pl.DeviceIdType.LOGICAL


def far_first():
    offsets = [(k >> 5, (k >> 3) & 3, (k >> 1) & 3, k & 1) for k in range(1, 128)]
    random.Random(1).shuffle(offsets)
    return sorted(offsets, key=lambda o: -sum(min(d, 4 - d) for d in o[:3]))


def signed_windows():
    row = lax.broadcasted_iota(jnp.int32, (2 * TURNS * NTAP, 128), 0)
    lane = lax.broadcasted_iota(jnp.int32, (2 * TURNS * NTAP, 128), 1)
    half, turn, tap = row // (TURNS * NTAP), (row // NTAP) % TURNS, row % NTAP
    pos = (tap * NFFT + turn * FOLD + half * 128 + lane).astype(jnp.float32)
    hann = 0.5 - 0.5 * jnp.cos(pos * (2.0 * math.pi / (NTAP * NFFT)))
    angle = (pos - 0.5 * NTAP * NFFT) * (math.pi / NFFT)
    middle = angle == 0.0
    sinc = jnp.where(middle, 1.0, jnp.sin(angle) / jnp.where(middle, 1.0, angle))
    return sinc * hann * (1 - 2 * (turn % 2)).astype(jnp.float32)


def first_columns():
    q = lax.broadcasted_iota(jnp.int32, (2 * CHANS, FOLD), 0)
    m = lax.broadcasted_iota(jnp.int32, (2 * CHANS, FOLD), 1)
    freq = q // 2 * STEP + STEP // 2
    phase = (m * freq + q % 2 * (NFFT // 4)) % NFFT
    return jnp.cos(phase.astype(jnp.float32) * (2.0 * math.pi / NFFT)) * (1.0 / math.sqrt(NFFT))


def spread_kernel(v_ref, r_ref, vbuf, wide, columns, folded, acc, tail, out, vsem, ssem, rsem, lsem):
    a, b = lax.axis_index("inp"), lax.axis_index("spec")
    me = a * 8 + b
    y, x_lo, core = lax.div(a, 4), lax.rem(lax.div(a, 2), 2), lax.rem(a, 2)
    x, z = lax.div(b, 4) * 2 + x_lo, lax.rem(b, 4)
    not_last = b < 7

    halves = [(0, HALF, 0, HALF), (HALF - NTAP + 1, FRAMES, HALF, FRAMES + NTAP - 1)]

    def v_copy(h, g):
        rows = pl.ds(pl.multiple_of(g * GROUP, GROUP), GROUP)
        lanes = pl.ds(h * HALF * NFFT, HALF * NFFT)
        return pltpu.make_async_copy(v_ref.at[rows, lanes], vbuf.at[rows, lanes], vsem.at[h, g])

    for h in range(2):
        for g in range(128 // GROUP):
            v_copy(h, g).start()

    barrier = pltpu.get_barrier_semaphore()

    def greet(k, carry):
        pl.semaphore_signal(barrier, inc=1, device_id=lax.rem(me + k, 128), device_id_type=LOGICAL)
        return carry

    lax.fori_loop(1, 128, greet, 0)
    tail[...] = jnp.zeros_like(tail)
    windows = signed_windows()
    for k in range(2 * TURNS * NTAP):
        wide[k] = jnp.broadcast_to(windows[k : k + 1, :], (8, 128))
    exact = first_columns()
    high = exact.astype(jnp.bfloat16)
    columns[:, 0:FOLD] = high
    columns[:, FOLD : 2 * FOLD] = high
    columns[:, 2 * FOLD :] = (exact - high.astype(jnp.float32)).astype(jnp.bfloat16)

    def fold(h, i):
        g, part = lax.div(i, 2), lax.rem(i, 2)
        f_begin, f_end, s_begin, s_end = halves[h]

        @pl.when(part == 0)
        def _():
            v_copy(h, g).wait()

        rows = pl.ds(pl.multiple_of(g * GROUP, GROUP), GROUP)
        sums = {}
        for f in range(f_begin, f_end):
            for u in range(TURNS):
                lanes = pl.ds(pl.multiple_of(f * NFFT + u * FOLD + part * 128, 128), 128)
                v = vbuf[rows, lanes].astype(jnp.float32).reshape(GROUP // 8, 8, 128)
                for t in range(NTAP):
                    s = f - t + NTAP - 1
                    if s_begin <= s < s_end:
                        term = v * wide[part * (TURNS * NTAP) + u * NTAP + t]
                        sums[s] = sums[s] + term if s in sums else term
            for s in [s for s in sums if s <= f or f == f_end - 1]:
                whole = sums.pop(s).reshape(GROUP, 128)
                high = whole.astype(jnp.bfloat16)
                low = (whole - high.astype(jnp.float32)).astype(jnp.bfloat16)
                folded[s - s_begin, rows, pl.ds(pl.multiple_of(part * 128, 128), 128)] = high
                folded[s - s_begin, rows, pl.ds(pl.multiple_of(part * 128 + FOLD, 128), 128)] = low

    def spectrum(n, count):
        frames = folded[pl.ds(n, count)].reshape(count * 128, 2 * FOLD)
        dims = (((1,), (1,)), ((), ()))
        got = lax.dot_general(columns[:, : 2 * FOLD], frames, dims, preferred_element_type=jnp.float32)
        got = got + lax.dot_general(columns[:, 2 * FOLD :], frames[:, :FOLD], dims, preferred_element_type=jnp.float32)
        return [got[:, k * 128 : (k + 1) * 128] for k in range(count)]

    def send(to, slabs, k):
        pltpu.make_async_remote_copy(
            src_ref=out.at[to, slabs],
            dst_ref=r_ref.at[me, slabs],
            send_sem=ssem.at[k],
            recv_sem=rsem.at[k],
            device_id=to,
            device_id_type=LOGICAL,
        ).start()

    parts = [pl.ds(0, 2), pl.ds(3, 2), pl.ds(2, 1)]

    def pack(to, h):
        for part in range(2):
            rows = pl.ds(pl.multiple_of((2 * to + part) * HALF, HALF), HALF)
            out[to, 3 * h + part] = acc[rows, :].astype(jnp.bfloat16)
        if h == 1:
            out[to, 2] = tail[pl.ds(pl.multiple_of(to * 8, 8), 8), :].astype(jnp.bfloat16)

    targets = []
    for dx, dy, dz, dc in far_first():
        x_to, y_to, z_to = lax.rem(x + dx, 4), lax.rem(y + dy, 4), lax.rem(z + dz, 4)
        targets.append(y_to * 32 + (lax.rem(x_to, 2) * 2 + lax.rem(core + dc, 2)) * 8 + lax.div(x_to, 2) * 4 + z_to)

    for h in range(2):

        def fold_step(i, carry):
            fold(h, i)
            return carry

        lax.fori_loop(0, 2 * (128 // GROUP), fold_step, 0)

        def main(n, carry):
            for k, got in enumerate(spectrum(2 * n, 2)):
                for g in range(2 * CHANS // 8):
                    acc[pl.ds(8 * g * HALF + 2 * n + k, 8, stride=HALF), :] = got[8 * g : 8 * g + 8]
            return carry

        lax.fori_loop(0, HALF // 2, main, 0)
        if h == 0:
            pl.semaphore_wait(barrier, 127)
        else:
            for k, got in enumerate(spectrum(HALF, NTAP - 1)):
                for g in range(2 * CHANS // 8):
                    tail[pl.ds(8 * g * 4 + k, 8, stride=4), :] = got[8 * g : 8 * g + 8]

        for n in range(0, 127, BATCH):
            batch = targets[n : n + BATCH]
            for to in batch:
                pack(to, h)
            for to in batch:
                send(to, parts[h], h)
            if h == 1:

                @pl.when(not_last)
                def _(batch=batch):
                    for to in batch:
                        send(to, parts[2], 2)

        pack(me, h)

    own = pltpu.make_async_copy(out.at[me], r_ref.at[me], lsem)
    own.start()
    own.wait()

    def landed(count, k, sem):
        block = r_ref.at[pl.ds(0, count), parts[k]]
        pltpu.make_async_copy(block, block, sem.at[k]).wait()

    for k in range(2):
        landed(127, k, ssem)
        landed(127, k, rsem)

    @pl.when(not_last)
    def _():
        landed(127, 2, ssem)
        landed(111, 2, rsem)

    @pl.when(jnp.logical_not(not_last))
    def _():
        landed(112, 2, rsem)


def spread(v):
    return pl.pallas_call(
        spread_kernel,
        out_shape=jax.ShapeDtypeStruct((128, 5, 8, 128), jnp.bfloat16),
        in_specs=[pl.BlockSpec(memory_space=pl.ANY)],
        out_specs=pl.BlockSpec(memory_space=pltpu.VMEM),
        scratch_shapes=[
            pltpu.VMEM((128, FRAMES * NFFT), jnp.bfloat16),
            pltpu.VMEM((2 * TURNS * NTAP, 8, 128), jnp.float32),
            pltpu.VMEM((2 * CHANS, 3 * FOLD), jnp.bfloat16),
            pltpu.VMEM((HALF + NTAP - 1, 128, 2 * FOLD), jnp.bfloat16),
            pltpu.VMEM((2 * CHANS * HALF, 128), jnp.float32),
            pltpu.VMEM((2 * CHANS * 4, 128), jnp.float32),
            pltpu.VMEM((CHANS, 5, 8, 128), jnp.bfloat16),
            pltpu.SemaphoreType.DMA((2, 128 // GROUP)),
            pltpu.SemaphoreType.DMA((3,)),
            pltpu.SemaphoreType.DMA((3,)),
            pltpu.SemaphoreType.DMA,
        ],
        compiler_params=pltpu.CompilerParams(collective_id=0, has_side_effects=True, vmem_limit_bytes=52 << 20),
        name="spread",
    )(v)


BLOCKS = 16
TILES = BLOCKS * (BLOCKS + 1) // 2


def tile_index(r, c):
    return r * BLOCKS - r * (r - 1) // 2 + (c - r)


def correlate_kernel(r_ref, o_ref, left, right, stage, sem):
    row = lax.broadcasted_iota(jnp.int32, (8, 128), 0)
    for c in range(BLOCKS):
        for part in range(2):
            for b in range(8):
                src = c * 8 + b
                head = r_ref[src, part].astype(jnp.float32)
                rest = r_ref[src, 3 + part].astype(jnp.float32)
                if b > 0:
                    terms = r_ref[src - 1, 2].astype(jnp.float32)
                    if part == 1:
                        terms = jnp.concatenate([terms[4:], terms[:4]], axis=0)
                    head = head + jnp.where(row < NTAP - 1, terms, 0.0)
                both = jnp.concatenate([head, rest], axis=0)
                at = part * 128 + b * 16
                right[c % 2, pl.ds(at, 16), 0:128] = both.astype(jnp.bfloat16)
        re, im = right[c % 2, 0:128, 0:128], right[c % 2, 128:256, 0:128]
        right[c % 2, 0:128, 128:256] = -im
        right[c % 2, 128:256, 128:256] = re
        left[c * 128 : (c + 1) * 128, 0:128] = re.T
        left[c * 128 : (c + 1) * 128, 128:256] = im.T
        got = jnp.dot(left[0 : (c + 1) * 128, :], right[c % 2], preferred_element_type=jnp.float32)
        for r in range(c + 1):
            t = tile_index(r, c)
            stage[t, 0] = got[r * 128 : (r + 1) * 128, 0:128] * (1.0 / 128)
            stage[t, 1] = got[r * 128 : (r + 1) * 128, 128:256] * (1.0 / 128)
        for r in range(c + 1):
            t = tile_index(r, c)
            pltpu.make_async_copy(stage.at[t], o_ref.at[t], sem).start()
    pltpu.make_async_copy(stage, o_ref, sem).wait()


def correlate(got):
    return pl.pallas_call(
        correlate_kernel,
        out_shape=jax.ShapeDtypeStruct((TILES, 2, TB, TB), jnp.float32),
        in_specs=[pl.BlockSpec(memory_space=pltpu.VMEM)],
        out_specs=pl.BlockSpec(memory_space=pl.ANY),
        scratch_shapes=[
            pltpu.VMEM((BLOCKS * 128, 256), jnp.bfloat16),
            pltpu.VMEM((2, 256, 256), jnp.bfloat16),
            pltpu.VMEM((TILES, 2, TB, TB), jnp.float32),
            pltpu.SemaphoreType.DMA,
        ],
        compiler_params=pltpu.CompilerParams(vmem_limit_bytes=40 << 20),
        name="correlate",
    )(got)


def shards(voltages):
    got = spread(voltages)
    return correlate(got)[None]


def solution(mesh):
    return jax.shard_map(
        shards,
        mesh=mesh,
        in_specs=(P("inp", "spec"),),
        out_specs=P(("inp", "spec"), None, None, None, None),
        check_vma=False,
    )
```

```python
import math
import random

import jax
import jax.numpy as jnp
from jax import lax
from jax.experimental import pallas as pl
from jax.experimental.pallas import tpu as pltpu
from jax.sharding import PartitionSpec as P

NFFT = 2048
NTAP = 4
TB = 128
CHANS = 128
STEP = 8
FRAMES = 16
HALF = FRAMES // 2
FOLD = 256
TURNS = NFFT // FOLD
GROUP = 32
BATCH = 16
LOGICAL = pl.DeviceIdType.LOGICAL


def far_first():
    offsets = [(k >> 5, (k >> 3) & 3, (k >> 1) & 3, k & 1) for k in range(1, 128)]
    random.Random(1).shuffle(offsets)
    return sorted(offsets, key=lambda o: -sum(min(d, 4 - d) for d in o[:3]))


def signed_windows():
    row = lax.broadcasted_iota(jnp.int32, (2 * TURNS * NTAP, 128), 0)
    lane = lax.broadcasted_iota(jnp.int32, (2 * TURNS * NTAP, 128), 1)
    half, turn, tap = row // (TURNS * NTAP), (row // NTAP) % TURNS, row % NTAP
    pos = (tap * NFFT + turn * FOLD + half * 128 + lane).astype(jnp.float32)
    hann = 0.5 - 0.5 * jnp.cos(pos * (2.0 * math.pi / (NTAP * NFFT)))
    angle = (pos - 0.5 * NTAP * NFFT) * (math.pi / NFFT)
    middle = angle == 0.0
    sinc = jnp.where(middle, 1.0, jnp.sin(angle) / jnp.where(middle, 1.0, angle))
    return sinc * hann * (1 - 2 * (turn % 2)).astype(jnp.float32)


def first_columns():
    q = lax.broadcasted_iota(jnp.int32, (2 * CHANS, FOLD), 0)
    m = lax.broadcasted_iota(jnp.int32, (2 * CHANS, FOLD), 1)
    freq = q // 2 * STEP + STEP // 2
    phase = (m * freq + q % 2 * (NFFT // 4)) % NFFT
    return jnp.cos(phase.astype(jnp.float32) * (2.0 * math.pi / NFFT)) * (1.0 / math.sqrt(NFFT))


def spread_kernel(v_ref, r_ref, vbuf, wide, columns, folded, acc, tail, out, vsem, ssem, rsem, lsem):
    a, b = lax.axis_index("inp"), lax.axis_index("spec")
    me = a * 8 + b
    y, x_lo, core = lax.div(a, 4), lax.rem(lax.div(a, 2), 2), lax.rem(a, 2)
    x, z = lax.div(b, 4) * 2 + x_lo, lax.rem(b, 4)
    not_last = b < 7

    stages = [(0, HALF, 0, HALF), (HALF - NTAP + 1, FRAMES, HALF, FRAMES), (FRAMES - NTAP + 1, FRAMES, FRAMES, FRAMES + NTAP - 1)]

    def v_copy(h, g):
        rows = pl.ds(pl.multiple_of(g * GROUP, GROUP), GROUP)
        lanes = pl.ds(h * HALF * NFFT, HALF * NFFT)
        return pltpu.make_async_copy(v_ref.at[rows, lanes], vbuf.at[rows, lanes], vsem.at[h, g])

    for h in range(2):
        for g in range(128 // GROUP):
            v_copy(h, g).start()

    barrier = pltpu.get_barrier_semaphore()

    def greet(k, carry):
        pl.semaphore_signal(barrier, inc=1, device_id=lax.rem(me + k, 128), device_id_type=LOGICAL)
        return carry

    lax.fori_loop(1, 128, greet, 0)
    tail[...] = jnp.zeros_like(tail)
    windows = signed_windows()
    for k in range(2 * TURNS * NTAP):
        wide[k] = jnp.broadcast_to(windows[k : k + 1, :], (8, 128))
    exact = first_columns()
    high = exact.astype(jnp.bfloat16)
    columns[:, 0:FOLD] = high
    columns[:, FOLD : 2 * FOLD] = high
    columns[:, 2 * FOLD :] = (exact - high.astype(jnp.float32)).astype(jnp.bfloat16)

    def fold(h, i):
        g, part = lax.div(i, 2), lax.rem(i, 2)
        f_begin, f_end, s_begin, s_end = stages[h]

        if h < 2:

            @pl.when(part == 0)
            def _():
                v_copy(h, g).wait()

        rows = pl.ds(pl.multiple_of(g * GROUP, GROUP), GROUP)
        sums = {}
        for f in range(f_begin, f_end):
            for u in range(TURNS):
                lanes = pl.ds(pl.multiple_of(f * NFFT + u * FOLD + part * 128, 128), 128)
                v = vbuf[rows, lanes].astype(jnp.float32).reshape(GROUP // 8, 8, 128)
                for t in range(NTAP):
                    s = f - t + NTAP - 1
                    if s_begin <= s < s_end:
                        term = v * wide[part * (TURNS * NTAP) + u * NTAP + t]
                        sums[s] = sums[s] + term if s in sums else term
            for s in [s for s in sums if s <= f or f == f_end - 1]:
                whole = sums.pop(s).reshape(GROUP, 128)
                high = whole.astype(jnp.bfloat16)
                low = (whole - high.astype(jnp.float32)).astype(jnp.bfloat16)
                folded[s - s_begin, rows, pl.ds(pl.multiple_of(part * 128, 128), 128)] = high
                folded[s - s_begin, rows, pl.ds(pl.multiple_of(part * 128 + FOLD, 128), 128)] = low

    def spectrum(n, count):
        frames = folded[pl.ds(n, count)].reshape(count * 128, 2 * FOLD)
        dims = (((1,), (1,)), ((), ()))
        got = lax.dot_general(columns[:, : 2 * FOLD], frames, dims, preferred_element_type=jnp.float32)
        got = got + lax.dot_general(columns[:, 2 * FOLD :], frames[:, :FOLD], dims, preferred_element_type=jnp.float32)
        return [got[:, k * 128 : (k + 1) * 128] for k in range(count)]

    def send(to, slabs, k):
        pltpu.make_async_remote_copy(
            src_ref=out.at[to, slabs],
            dst_ref=r_ref.at[me, slabs],
            send_sem=ssem.at[k],
            recv_sem=rsem.at[k],
            device_id=to,
            device_id_type=LOGICAL,
        ).start()

    parts = [pl.ds(0, 2), pl.ds(3, 2), pl.ds(2, 1)]

    def pack(to, h):
        if h == 2:
            out[to, 2] = tail[pl.ds(pl.multiple_of(to * 8, 8), 8), :].astype(jnp.bfloat16)
            return
        for part in range(2):
            rows = pl.ds(pl.multiple_of((2 * to + part) * HALF, HALF), HALF)
            out[to, 3 * h + part] = acc[rows, :].astype(jnp.bfloat16)

    def deliver(h):
        for n in range(0, 127, BATCH):
            batch = targets[n : n + BATCH]
            for to in batch:
                pack(to, h)
            for to in batch:
                send(to, parts[h], h)
        pack(me, h)

    targets = []
    for dx, dy, dz, dc in far_first():
        x_to, y_to, z_to = lax.rem(x + dx, 4), lax.rem(y + dy, 4), lax.rem(z + dz, 4)
        targets.append(y_to * 32 + (lax.rem(x_to, 2) * 2 + lax.rem(core + dc, 2)) * 8 + lax.div(x_to, 2) * 4 + z_to)

    def stage(h):
        def fold_step(i, carry):
            fold(h, i)
            return carry

        lax.fori_loop(0, 2 * (128 // GROUP), fold_step, 0)
        if h < 2:
            for n in range(0, HALF, 2):
                for k, got in enumerate(spectrum(n, 2)):
                    for g in range(2 * CHANS // 8):
                        acc[pl.ds(8 * g * HALF + n + k, 8, stride=HALF), :] = got[8 * g : 8 * g + 8]
        else:
            for k, got in enumerate(spectrum(0, NTAP - 1)):
                for g in range(2 * CHANS // 8):
                    tail[pl.ds(8 * g * 4 + k, 8, stride=4), :] = got[8 * g : 8 * g + 8]
        if h == 0:
            pl.semaphore_wait(barrier, 127)
        deliver(h)

    stage(0)
    stage(1)
    pl.when(not_last)(lambda: stage(2))

    own = pltpu.make_async_copy(out.at[me], r_ref.at[me], lsem)
    own.start()
    own.wait()

    def landed(count, k, sem):
        block = r_ref.at[pl.ds(0, count), parts[k]]
        pltpu.make_async_copy(block, block, sem.at[k]).wait()

    for k in range(2):
        landed(127, k, ssem)
        landed(127, k, rsem)

    @pl.when(not_last)
    def _():
        landed(127, 2, ssem)
        landed(111, 2, rsem)

    @pl.when(jnp.logical_not(not_last))
    def _():
        landed(112, 2, rsem)


def spread(v):
    return pl.pallas_call(
        spread_kernel,
        out_shape=jax.ShapeDtypeStruct((128, 5, 8, 128), jnp.bfloat16),
        in_specs=[pl.BlockSpec(memory_space=pl.ANY)],
        out_specs=pl.BlockSpec(memory_space=pltpu.VMEM),
        scratch_shapes=[
            pltpu.VMEM((128, FRAMES * NFFT), jnp.bfloat16),
            pltpu.VMEM((2 * TURNS * NTAP, 8, 128), jnp.float32),
            pltpu.VMEM((2 * CHANS, 3 * FOLD), jnp.bfloat16),
            pltpu.VMEM((HALF, 128, 2 * FOLD), jnp.bfloat16),
            pltpu.VMEM((2 * CHANS * HALF, 128), jnp.float32),
            pltpu.VMEM((2 * CHANS * 4, 128), jnp.float32),
            pltpu.VMEM((CHANS, 5, 8, 128), jnp.bfloat16),
            pltpu.SemaphoreType.DMA((2, 128 // GROUP)),
            pltpu.SemaphoreType.DMA((3,)),
            pltpu.SemaphoreType.DMA((3,)),
            pltpu.SemaphoreType.DMA,
        ],
        compiler_params=pltpu.CompilerParams(collective_id=0, has_side_effects=True, vmem_limit_bytes=52 << 20),
        name="spread",
    )(v)


BLOCKS = 16
TILES = BLOCKS * (BLOCKS + 1) // 2


def tile_index(r, c):
    return r * BLOCKS - r * (r - 1) // 2 + (c - r)


def correlate_kernel(r_ref, o_ref, left, right, stage, sem):
    row = lax.broadcasted_iota(jnp.int32, (8, 128), 0)
    for c in range(BLOCKS):
        for part in range(2):
            for b in range(8):
                src = c * 8 + b
                head = r_ref[src, part].astype(jnp.float32)
                rest = r_ref[src, 3 + part].astype(jnp.float32)
                if b > 0:
                    terms = r_ref[src - 1, 2].astype(jnp.float32)
                    if part == 1:
                        terms = jnp.concatenate([terms[4:], terms[:4]], axis=0)
                    head = head + jnp.where(row < NTAP - 1, terms, 0.0)
                both = jnp.concatenate([head, rest], axis=0)
                at = part * 128 + b * 16
                right[c % 2, pl.ds(at, 16), 0:128] = both.astype(jnp.bfloat16)
        re, im = right[c % 2, 0:128, 0:128], right[c % 2, 128:256, 0:128]
        right[c % 2, 0:128, 128:256] = -im
        right[c % 2, 128:256, 128:256] = re
        left[c * 128 : (c + 1) * 128, 0:128] = re.T
        left[c * 128 : (c + 1) * 128, 128:256] = im.T
        got = jnp.dot(left[0 : (c + 1) * 128, :], right[c % 2], preferred_element_type=jnp.float32)
        for r in range(c + 1):
            t = tile_index(r, c)
            stage[t, 0] = got[r * 128 : (r + 1) * 128, 0:128] * (1.0 / 128)
            stage[t, 1] = got[r * 128 : (r + 1) * 128, 128:256] * (1.0 / 128)
        for r in range(c + 1):
            t = tile_index(r, c)
            pltpu.make_async_copy(stage.at[t], o_ref.at[t], sem).start()
    pltpu.make_async_copy(stage, o_ref, sem).wait()


def correlate(got):
    return pl.pallas_call(
        correlate_kernel,
        out_shape=jax.ShapeDtypeStruct((TILES, 2, TB, TB), jnp.float32),
        in_specs=[pl.BlockSpec(memory_space=pltpu.VMEM)],
        out_specs=pl.BlockSpec(memory_space=pl.ANY),
        scratch_shapes=[
            pltpu.VMEM((BLOCKS * 128, 256), jnp.bfloat16),
            pltpu.VMEM((2, 256, 256), jnp.bfloat16),
            pltpu.VMEM((TILES, 2, TB, TB), jnp.float32),
            pltpu.SemaphoreType.DMA,
        ],
        compiler_params=pltpu.CompilerParams(vmem_limit_bytes=40 << 20),
        name="correlate",
    )(got)


def shards(voltages):
    got = spread(voltages)
    return correlate(got)[None]


def solution(mesh):
    return jax.shard_map(
        shards,
        mesh=mesh,
        in_specs=(P("inp", "spec"),),
        out_specs=P(("inp", "spec"), None, None, None, None),
        check_vma=False,
    )
```

```python
import functools
import math
import random

import jax
import jax.numpy as jnp
from jax import lax
from jax.experimental import pallas as pl
from jax.experimental.pallas import tpu as pltpu
from jax.sharding import PartitionSpec as P

NFFT = 2048
NTAP = 4
TB = 128
CHANS = 128
STEP = 8
FRAMES = 16
HALF = FRAMES // 2
FOLD = 256
TURNS = NFFT // FOLD
GROUP = 32
BATCH = 16
Z_LEAD, Y_LEAD, X_LEAD = 0.5, 0.2, 0.1
LOGICAL = pl.DeviceIdType.LOGICAL


def order():
    places = [(k >> 5, (k >> 3) & 3, (k >> 1) & 3, k & 1) for k in range(128)]
    draw = random.Random(1)
    key = {o: draw.random() + Z_LEAD * o[2] / 3 + Y_LEAD * o[1] / 3 - X_LEAD * min(o[0], 4 - o[0]) for o in places}
    return sorted(places, key=key.get)


def signed_windows():
    row = lax.broadcasted_iota(jnp.int32, (2 * TURNS * NTAP, 128), 0)
    lane = lax.broadcasted_iota(jnp.int32, (2 * TURNS * NTAP, 128), 1)
    half, turn, tap = row // (TURNS * NTAP), (row // NTAP) % TURNS, row % NTAP
    pos = (tap * NFFT + turn * FOLD + half * 128 + lane).astype(jnp.float32)
    hann = 0.5 - 0.5 * jnp.cos(pos * (2.0 * math.pi / (NTAP * NFFT)))
    angle = (pos - 0.5 * NTAP * NFFT) * (math.pi / NFFT)
    middle = angle == 0.0
    sinc = jnp.where(middle, 1.0, jnp.sin(angle) / jnp.where(middle, 1.0, angle))
    return sinc * hann * (1 - 2 * (turn % 2)).astype(jnp.float32)


def first_columns():
    q = lax.broadcasted_iota(jnp.int32, (2 * CHANS, FOLD), 0)
    m = lax.broadcasted_iota(jnp.int32, (2 * CHANS, FOLD), 1)
    freq = q // 2 * STEP + STEP // 2
    phase = (m * freq + q % 2 * (NFFT // 4)) % NFFT
    return jnp.cos(phase.astype(jnp.float32) * (2.0 * math.pi / NFFT)) * (1.0 / math.sqrt(NFFT))


def spread_kernel(v_ref, r_ref, vbuf, wide, columns, folded, acc, tail, out, vsem, ssem, rsem, lsem):
    a, b = lax.axis_index("inp"), lax.axis_index("spec")
    me = a * 8 + b
    y, x_lo, core = lax.div(a, 4), lax.rem(lax.div(a, 2), 2), lax.rem(a, 2)
    x, z = lax.div(b, 4) * 2 + x_lo, lax.rem(b, 4)
    not_last = b < 7

    stages = [(0, HALF, 0, HALF), (HALF - NTAP + 1, FRAMES, HALF, FRAMES), (FRAMES - NTAP + 1, FRAMES, FRAMES, FRAMES + NTAP - 1)]

    def v_copy(h, g):
        rows = pl.ds(pl.multiple_of(g * GROUP, GROUP), GROUP)
        lanes = pl.ds(h * HALF * NFFT, HALF * NFFT)
        return pltpu.make_async_copy(v_ref.at[rows, lanes], vbuf.at[rows, lanes], vsem.at[h, g])

    for h in range(2):
        for g in range(128 // GROUP):
            v_copy(h, g).start()

    barrier = pltpu.get_barrier_semaphore()

    def greet(k, carry):
        pl.semaphore_signal(barrier, inc=1, device_id=lax.rem(me + k, 128), device_id_type=LOGICAL)
        return carry

    lax.fori_loop(1, 128, greet, 0, unroll=127)
    tail[...] = jnp.zeros_like(tail)
    windows = signed_windows()
    for k in range(2 * TURNS * NTAP):
        wide[k] = jnp.broadcast_to(windows[k : k + 1, :], (8, 128))
    exact = first_columns()
    high = exact.astype(jnp.bfloat16)
    columns[:, 0:FOLD] = high
    columns[:, FOLD : 2 * FOLD] = high
    columns[:, 2 * FOLD :] = (exact - high.astype(jnp.float32)).astype(jnp.bfloat16)

    def fold(h, i):
        g, part = lax.div(i, 2), lax.rem(i, 2)
        f_begin, f_end, s_begin, s_end = stages[h]

        if h < 2:

            @pl.when(part == 0)
            def _():
                v_copy(h, g).wait()

        rows = pl.ds(pl.multiple_of(g * GROUP, GROUP), GROUP)
        sums = {}
        for f in range(f_begin, f_end):
            for u in range(TURNS):
                lanes = pl.ds(pl.multiple_of(f * NFFT + u * FOLD + part * 128, 128), 128)
                v = vbuf[rows, lanes].astype(jnp.float32).reshape(GROUP // 8, 8, 128)
                for t in range(NTAP):
                    s = f - t + NTAP - 1
                    if s_begin <= s < s_end:
                        term = v * wide[part * (TURNS * NTAP) + u * NTAP + t]
                        sums[s] = sums[s] + term if s in sums else term
            for s in [s for s in sums if s <= f or f == f_end - 1]:
                whole = sums.pop(s).reshape(GROUP, 128)
                high = whole.astype(jnp.bfloat16)
                low = (whole - high.astype(jnp.float32)).astype(jnp.bfloat16)
                folded[s - s_begin, rows, pl.ds(pl.multiple_of(part * 128, 128), 128)] = high
                folded[s - s_begin, rows, pl.ds(pl.multiple_of(part * 128 + FOLD, 128), 128)] = low

    def spectrum(n, count):
        frames = folded[pl.ds(n, count)].reshape(count * 128, 2 * FOLD)
        dims = (((1,), (1,)), ((), ()))
        got = lax.dot_general(columns[:, : 2 * FOLD], frames, dims, preferred_element_type=jnp.float32)
        got = got + lax.dot_general(columns[:, 2 * FOLD :], frames[:, :FOLD], dims, preferred_element_type=jnp.float32)
        return [got[:, k * 128 : (k + 1) * 128] for k in range(count)]

    def send(to, slabs, k):
        pltpu.make_async_remote_copy(
            src_ref=out.at[to, slabs],
            dst_ref=r_ref.at[me, slabs],
            send_sem=ssem.at[k],
            recv_sem=rsem.at[k],
            device_id=to,
            device_id_type=LOGICAL,
        ).start()

    parts = [pl.ds(0, 2), pl.ds(3, 2), pl.ds(2, 1)]

    def pack(to, h):
        if h == 2:
            out[to, 2] = tail[pl.ds(pl.multiple_of(to * 8, 8), 8), :].astype(jnp.bfloat16)
            return
        for part in range(2):
            rows = pl.ds(pl.multiple_of((2 * to + part) * HALF, HALF), HALF)
            out[to, 3 * h + part] = acc[h, rows, :].astype(jnp.bfloat16)

    def deliver(*which):
        for n in range(0, 128, BATCH):
            batch = targets[n : n + BATCH]
            for to, _ in batch:
                for h in which:
                    pack(to, h)
            for h in which:

                def go(batch=batch, h=h):
                    for to, maybe_own in batch:
                        if maybe_own:
                            pl.when(to != me)(functools.partial(send, to, parts[h], h))
                        else:
                            send(to, parts[h], h)

                if h == 2:
                    pl.when(not_last)(go)
                else:
                    go()

    targets = []
    for dx, y_to, z_to, dc in order():
        x_to = lax.rem(x + dx, 4)
        to = y_to * 32 + (lax.rem(x_to, 2) * 2 + lax.rem(core + dc, 2)) * 8 + lax.div(x_to, 2) * 4 + z_to
        targets.append((to, dx == 0 and dc == 0))

    def stage(h):
        def fold_step(i, carry):
            fold(h, i)
            return carry

        lax.fori_loop(0, 2 * (128 // GROUP), fold_step, 0)
        if h < 2:
            for n in range(0, HALF, 2):
                for k, got in enumerate(spectrum(n, 2)):
                    for g in range(2 * CHANS // 8):
                        acc[h, pl.ds(8 * g * HALF + n + k, 8, stride=HALF), :] = got[8 * g : 8 * g + 8]
        else:
            for k, got in enumerate(spectrum(0, NTAP - 1)):
                for g in range(2 * CHANS // 8):
                    tail[pl.ds(8 * g * 4 + k, 8, stride=4), :] = got[8 * g : 8 * g + 8]

    stage(0)
    pl.semaphore_wait(barrier, 127)
    deliver(0)
    stage(1)
    pl.when(not_last)(lambda: stage(2))
    deliver(1, 2)

    own = pltpu.make_async_copy(out.at[me], r_ref.at[me], lsem)
    own.start()
    own.wait()

    def landed(count, k, sem):
        block = r_ref.at[pl.ds(0, count), parts[k]]
        pltpu.make_async_copy(block, block, sem.at[k]).wait()

    for k in range(2):
        landed(127, k, ssem)
        landed(127, k, rsem)

    @pl.when(not_last)
    def _():
        landed(127, 2, ssem)
        landed(111, 2, rsem)

    @pl.when(jnp.logical_not(not_last))
    def _():
        landed(112, 2, rsem)


def spread(v):
    return pl.pallas_call(
        spread_kernel,
        out_shape=jax.ShapeDtypeStruct((128, 5, 8, 128), jnp.bfloat16),
        in_specs=[pl.BlockSpec(memory_space=pl.ANY)],
        out_specs=pl.BlockSpec(memory_space=pltpu.VMEM),
        scratch_shapes=[
            pltpu.VMEM((128, FRAMES * NFFT), jnp.bfloat16),
            pltpu.VMEM((2 * TURNS * NTAP, 8, 128), jnp.float32),
            pltpu.VMEM((2 * CHANS, 3 * FOLD), jnp.bfloat16),
            pltpu.VMEM((HALF, 128, 2 * FOLD), jnp.bfloat16),
            pltpu.VMEM((2, 2 * CHANS * HALF, 128), jnp.float32),
            pltpu.VMEM((2 * CHANS * 4, 128), jnp.float32),
            pltpu.VMEM((CHANS, 5, 8, 128), jnp.bfloat16),
            pltpu.SemaphoreType.DMA((2, 128 // GROUP)),
            pltpu.SemaphoreType.DMA((3,)),
            pltpu.SemaphoreType.DMA((3,)),
            pltpu.SemaphoreType.DMA,
        ],
        compiler_params=pltpu.CompilerParams(collective_id=0, has_side_effects=True, vmem_limit_bytes=52 << 20),
        name="spread",
    )(v)


BLOCKS = 16
TILES = BLOCKS * (BLOCKS + 1) // 2


def tile_index(r, c):
    return r * BLOCKS - r * (r - 1) // 2 + (c - r)


def correlate_kernel(r_ref, o_ref, left, right, stage, sem):
    row = lax.broadcasted_iota(jnp.int32, (8, 128), 0)
    for c in range(BLOCKS):
        for part in range(2):
            for b in range(8):
                src = c * 8 + b
                head = r_ref[src, part].astype(jnp.float32)
                rest = r_ref[src, 3 + part].astype(jnp.float32)
                if b > 0:
                    terms = r_ref[src - 1, 2].astype(jnp.float32)
                    if part == 1:
                        terms = jnp.concatenate([terms[4:], terms[:4]], axis=0)
                    head = head + jnp.where(row < NTAP - 1, terms, 0.0)
                both = jnp.concatenate([head, rest], axis=0)
                at = part * 128 + b * 16
                right[c % 2, pl.ds(at, 16), 0:128] = both.astype(jnp.bfloat16)
        re, im = right[c % 2, 0:128, 0:128], right[c % 2, 128:256, 0:128]
        right[c % 2, 0:128, 128:256] = -im
        right[c % 2, 128:256, 128:256] = re
        left[c * 128 : (c + 1) * 128, 0:128] = re.T
        left[c * 128 : (c + 1) * 128, 128:256] = im.T
        got = jnp.dot(left[0 : (c + 1) * 128, :], right[c % 2], preferred_element_type=jnp.float32)
        for r in range(c + 1):
            t = tile_index(r, c)
            stage[t, 0] = got[r * 128 : (r + 1) * 128, 0:128] * (1.0 / 128)
            stage[t, 1] = got[r * 128 : (r + 1) * 128, 128:256] * (1.0 / 128)
        for r in range(c + 1):
            t = tile_index(r, c)
            for part in range(2):
                pltpu.make_async_copy(stage.at[t, part], o_ref.at[t, part], sem).start()
    pltpu.make_async_copy(stage, o_ref, sem).wait()


def correlate(got):
    return pl.pallas_call(
        correlate_kernel,
        out_shape=jax.ShapeDtypeStruct((TILES, 2, TB, TB), jnp.float32),
        in_specs=[pl.BlockSpec(memory_space=pltpu.VMEM)],
        out_specs=pl.BlockSpec(memory_space=pl.ANY),
        scratch_shapes=[
            pltpu.VMEM((BLOCKS * 128, 256), jnp.bfloat16),
            pltpu.VMEM((2, 256, 256), jnp.bfloat16),
            pltpu.VMEM((TILES, 2, TB, TB), jnp.float32),
            pltpu.SemaphoreType.DMA,
        ],
        compiler_params=pltpu.CompilerParams(vmem_limit_bytes=40 << 20),
        name="correlate",
    )(got)


def shards(voltages):
    got = spread(voltages)
    return correlate(got)[None]


def solution(mesh):
    return jax.shard_map(
        shards,
        mesh=mesh,
        in_specs=(P("inp", "spec"),),
        out_specs=P(("inp", "spec"), None, None, None, None),
        check_vma=False,
    )
```

```python
import functools
import math
import random

import jax
import jax.numpy as jnp
from jax import lax
from jax.experimental import pallas as pl
from jax.experimental.pallas import tpu as pltpu
from jax.sharding import PartitionSpec as P

NFFT = 2048
NTAP = 4
TB = 128
CHANS = 128
STEP = 8
FRAMES = 16
HALF = FRAMES // 2
FOLD = 256
TURNS = NFFT // FOLD
GROUP = 32
BATCH = 8
Z_LEAD, Y_LEAD, X_LEAD = 0.5, 0.2, 0.1
LOGICAL = pl.DeviceIdType.LOGICAL


def order():
    places = [(k >> 5, (k >> 3) & 3, (k >> 1) & 3, k & 1) for k in range(128)]
    draw = random.Random(1)
    key = {o: draw.random() + Z_LEAD * o[2] / 3 + Y_LEAD * o[1] / 3 - X_LEAD * min(o[0], 4 - o[0]) for o in places}
    return sorted(places, key=key.get)


def signed_windows():
    row = lax.broadcasted_iota(jnp.int32, (2 * TURNS * NTAP, 128), 0)
    lane = lax.broadcasted_iota(jnp.int32, (2 * TURNS * NTAP, 128), 1)
    half, turn, tap = row // (TURNS * NTAP), (row // NTAP) % TURNS, row % NTAP
    pos = (tap * NFFT + turn * FOLD + half * 128 + lane).astype(jnp.float32)
    hann = 0.5 - 0.5 * jnp.cos(pos * (2.0 * math.pi / (NTAP * NFFT)))
    angle = (pos - 0.5 * NTAP * NFFT) * (math.pi / NFFT)
    middle = angle == 0.0
    sinc = jnp.where(middle, 1.0, jnp.sin(angle) / jnp.where(middle, 1.0, angle))
    return sinc * hann * (1 - 2 * (turn % 2)).astype(jnp.float32)


def first_columns():
    q = lax.broadcasted_iota(jnp.int32, (2 * CHANS, FOLD), 0)
    m = lax.broadcasted_iota(jnp.int32, (2 * CHANS, FOLD), 1)
    freq = q // 2 * STEP + STEP // 2
    phase = (m * freq + q % 2 * (NFFT // 4)) % NFFT
    return jnp.cos(phase.astype(jnp.float32) * (2.0 * math.pi / NFFT)) * (1.0 / math.sqrt(NFFT))


def spread_kernel(v_ref, r_ref, vbuf, wide, columns, folded, acc, tail, out, vsem, ssem, rsem, lsem):
    a, b = lax.axis_index("inp"), lax.axis_index("spec")
    me = a * 8 + b
    y, x_lo, core = lax.div(a, 4), lax.rem(lax.div(a, 2), 2), lax.rem(a, 2)
    x, z = lax.div(b, 4) * 2 + x_lo, lax.rem(b, 4)
    not_last = b < 7

    stages = [(0, HALF, 0, HALF), (HALF - NTAP + 1, FRAMES, HALF, FRAMES), (FRAMES - NTAP + 1, FRAMES, FRAMES, FRAMES + NTAP - 1)]

    def v_copy(h, g):
        rows = pl.ds(pl.multiple_of(g * GROUP, GROUP), GROUP)
        lanes = pl.ds(h * HALF * NFFT, HALF * NFFT)
        return pltpu.make_async_copy(v_ref.at[rows, lanes], vbuf.at[rows, lanes], vsem.at[h, g])

    for h in range(2):
        for g in range(128 // GROUP):
            v_copy(h, g).start()

    barrier = pltpu.get_barrier_semaphore()

    def greet(k, carry):
        pl.semaphore_signal(barrier, inc=1, device_id=lax.rem(me + k, 128), device_id_type=LOGICAL)
        return carry

    lax.fori_loop(1, 128, greet, 0, unroll=127)
    tail[...] = jnp.zeros_like(tail)
    windows = signed_windows()
    for k in range(2 * TURNS * NTAP):
        wide[k] = jnp.broadcast_to(windows[k : k + 1, :], (8, 128))
    exact = first_columns()
    high = exact.astype(jnp.bfloat16)
    columns[:, 0:FOLD] = high
    columns[:, FOLD : 2 * FOLD] = high
    columns[:, 2 * FOLD :] = (exact - high.astype(jnp.float32)).astype(jnp.bfloat16)

    def fold(h, i):
        g, part = lax.div(i, 2), lax.rem(i, 2)
        f_begin, f_end, s_begin, s_end = stages[h]

        if h < 2:

            @pl.when(part == 0)
            def _():
                v_copy(h, g).wait()

        rows = pl.ds(pl.multiple_of(g * GROUP, GROUP), GROUP)
        sums = {}
        for f in range(f_begin, f_end):
            for u in range(TURNS):
                lanes = pl.ds(pl.multiple_of(f * NFFT + u * FOLD + part * 128, 128), 128)
                v = vbuf[rows, lanes].astype(jnp.float32).reshape(GROUP // 8, 8, 128)
                for t in range(NTAP):
                    s = f - t + NTAP - 1
                    if s_begin <= s < s_end:
                        term = v * wide[part * (TURNS * NTAP) + u * NTAP + t]
                        sums[s] = sums[s] + term if s in sums else term
            for s in [s for s in sums if s <= f or f == f_end - 1]:
                whole = sums.pop(s).reshape(GROUP, 128)
                high = whole.astype(jnp.bfloat16)
                low = (whole - high.astype(jnp.float32)).astype(jnp.bfloat16)
                folded[s - s_begin, rows, pl.ds(pl.multiple_of(part * 128, 128), 128)] = high
                folded[s - s_begin, rows, pl.ds(pl.multiple_of(part * 128 + FOLD, 128), 128)] = low

    def spectrum(n, count):
        frames = folded[pl.ds(n, count)].reshape(count * 128, 2 * FOLD)
        dims = (((1,), (1,)), ((), ()))
        got = lax.dot_general(columns[:, : 2 * FOLD], frames, dims, preferred_element_type=jnp.float32)
        got = got + lax.dot_general(columns[:, 2 * FOLD :], frames[:, :FOLD], dims, preferred_element_type=jnp.float32)
        return [got[:, k * 128 : (k + 1) * 128] for k in range(count)]

    def send(to, slabs, k):
        pltpu.make_async_remote_copy(
            src_ref=out.at[to, slabs],
            dst_ref=r_ref.at[me, slabs],
            send_sem=ssem.at[k],
            recv_sem=rsem.at[k],
            device_id=to,
            device_id_type=LOGICAL,
        ).start()

    parts = [pl.ds(0, 2), pl.ds(3, 2), pl.ds(2, 1)]

    def pack(to, h):
        if h == 2:
            out[to, 2] = tail[pl.ds(pl.multiple_of(to * 8, 8), 8), :].astype(jnp.bfloat16)
            return
        for part in range(2):
            rows = pl.ds(pl.multiple_of((2 * to + part) * HALF, HALF), HALF)
            out[to, 3 * h + part] = acc[h, rows, :].astype(jnp.bfloat16)

    def deliver(*which):
        for n in range(0, 128, BATCH):
            batch = targets[n : n + BATCH]
            for to, _ in batch:
                for h in which:
                    pack(to, h)
            for h in which:

                def go(batch=batch, h=h):
                    for to, maybe_own in batch:
                        if maybe_own:
                            pl.when(to != me)(functools.partial(send, to, parts[h], h))
                        else:
                            send(to, parts[h], h)

                if h == 2:
                    pl.when(not_last)(go)
                else:
                    go()

    targets = []
    for dx, y_to, z_to, dc in order():
        x_to = lax.rem(x + dx, 4)
        to = y_to * 32 + (lax.rem(x_to, 2) * 2 + lax.rem(core + dc, 2)) * 8 + lax.div(x_to, 2) * 4 + z_to
        targets.append((to, dx == 0 and dc == 0))

    def stage(h):
        def fold_step(i, carry):
            fold(h, i)
            return carry

        lax.fori_loop(0, 2 * (128 // GROUP), fold_step, 0)
        if h < 2:
            for n in range(0, HALF, 2):
                for k, got in enumerate(spectrum(n, 2)):
                    for g in range(2 * CHANS // 8):
                        acc[h, pl.ds(8 * g * HALF + n + k, 8, stride=HALF), :] = got[8 * g : 8 * g + 8]
        else:
            for k, got in enumerate(spectrum(0, NTAP - 1)):
                for g in range(2 * CHANS // 8):
                    tail[pl.ds(8 * g * 4 + k, 8, stride=4), :] = got[8 * g : 8 * g + 8]

    stage(0)
    pl.semaphore_wait(barrier, 127)
    deliver(0)
    stage(1)
    pl.when(not_last)(lambda: stage(2))
    deliver(1, 2)

    own = pltpu.make_async_copy(out.at[me], r_ref.at[me], lsem)
    own.start()
    own.wait()

    def landed(count, k, sem):
        block = r_ref.at[pl.ds(0, count), parts[k]]
        pltpu.make_async_copy(block, block, sem.at[k]).wait()

    for k in range(2):
        landed(127, k, ssem)
        landed(127, k, rsem)

    @pl.when(not_last)
    def _():
        landed(127, 2, ssem)
        landed(111, 2, rsem)

    @pl.when(jnp.logical_not(not_last))
    def _():
        landed(112, 2, rsem)


def spread(v):
    return pl.pallas_call(
        spread_kernel,
        out_shape=jax.ShapeDtypeStruct((128, 5, 8, 128), jnp.bfloat16),
        in_specs=[pl.BlockSpec(memory_space=pl.ANY)],
        out_specs=pl.BlockSpec(memory_space=pltpu.VMEM),
        scratch_shapes=[
            pltpu.VMEM((128, FRAMES * NFFT), jnp.bfloat16),
            pltpu.VMEM((2 * TURNS * NTAP, 8, 128), jnp.float32),
            pltpu.VMEM((2 * CHANS, 3 * FOLD), jnp.bfloat16),
            pltpu.VMEM((HALF, 128, 2 * FOLD), jnp.bfloat16),
            pltpu.VMEM((2, 2 * CHANS * HALF, 128), jnp.float32),
            pltpu.VMEM((2 * CHANS * 4, 128), jnp.float32),
            pltpu.VMEM((CHANS, 5, 8, 128), jnp.bfloat16),
            pltpu.SemaphoreType.DMA((2, 128 // GROUP)),
            pltpu.SemaphoreType.DMA((3,)),
            pltpu.SemaphoreType.DMA((3,)),
            pltpu.SemaphoreType.DMA,
        ],
        compiler_params=pltpu.CompilerParams(collective_id=0, has_side_effects=True, vmem_limit_bytes=52 << 20),
        name="spread",
    )(v)


BLOCKS = 16
TILES = BLOCKS * (BLOCKS + 1) // 2


def tile_index(r, c):
    return r * BLOCKS - r * (r - 1) // 2 + (c - r)


def correlate_kernel(r_ref, o_ref, left, right, stage, sem):
    row = lax.broadcasted_iota(jnp.int32, (8, 128), 0)
    for c in range(BLOCKS):
        for part in range(2):
            for b in range(8):
                src = c * 8 + b
                head = r_ref[src, part].astype(jnp.float32)
                rest = r_ref[src, 3 + part].astype(jnp.float32)
                if b > 0:
                    terms = r_ref[src - 1, 2].astype(jnp.float32)
                    if part == 1:
                        terms = jnp.concatenate([terms[4:], terms[:4]], axis=0)
                    head = head + jnp.where(row < NTAP - 1, terms, 0.0)
                both = jnp.concatenate([head, rest], axis=0)
                at = part * 128 + b * 16
                right[c % 2, pl.ds(at, 16), 0:128] = both.astype(jnp.bfloat16)
        re, im = right[c % 2, 0:128, 0:128], right[c % 2, 128:256, 0:128]
        right[c % 2, 0:128, 128:256] = -im
        right[c % 2, 128:256, 128:256] = re
        left[c * 128 : (c + 1) * 128, 0:128] = re.T
        left[c * 128 : (c + 1) * 128, 128:256] = im.T
        got = jnp.dot(left[0 : (c + 1) * 128, :], right[c % 2], preferred_element_type=jnp.float32)
        for r in range(c + 1):
            t = tile_index(r, c)
            stage[t, 0] = got[r * 128 : (r + 1) * 128, 0:128] * (1.0 / 128)
            stage[t, 1] = got[r * 128 : (r + 1) * 128, 128:256] * (1.0 / 128)
        for r in range(c + 1):
            t = tile_index(r, c)
            for part in range(2):
                pltpu.make_async_copy(stage.at[t, part], o_ref.at[t, part], sem).start()
    pltpu.make_async_copy(stage, o_ref, sem).wait()


def correlate(got):
    return pl.pallas_call(
        correlate_kernel,
        out_shape=jax.ShapeDtypeStruct((TILES, 2, TB, TB), jnp.float32),
        in_specs=[pl.BlockSpec(memory_space=pltpu.VMEM)],
        out_specs=pl.BlockSpec(memory_space=pl.ANY),
        scratch_shapes=[
            pltpu.VMEM((BLOCKS * 128, 256), jnp.bfloat16),
            pltpu.VMEM((2, 256, 256), jnp.bfloat16),
            pltpu.VMEM((TILES, 2, TB, TB), jnp.float32),
            pltpu.SemaphoreType.DMA,
        ],
        compiler_params=pltpu.CompilerParams(vmem_limit_bytes=40 << 20),
        name="correlate",
    )(got)


def shards(voltages):
    got = spread(voltages)
    return correlate(got)[None]


def solution(mesh):
    return jax.shard_map(
        shards,
        mesh=mesh,
        in_specs=(P("inp", "spec"),),
        out_specs=P(("inp", "spec"), None, None, None, None),
        check_vma=False,
    )
```
